32 devices in a mesh: expert: 2 (over y), blk: 16 (over z, x, core).
Axes of the slice: x: 2, y: 2, z: 4, core: 2. Of those that a mesh axis runs over, the one named last changes fastest.
Arguments:
- query_grads: bfloat16 [2, 16384, 2304], P('expert', 'blk'), may hold values from -0.125 to 0.125
- train_grads: bfloat16 [2, 128, 2304], P('expert', 'blk'), may hold values from -6 to 6
- counts: int32 [2, 128], P('expert', 'blk'), may hold values from 0 to 64
- factor: bfloat16 [2, 2304, 2304], P('expert', 'blk'), as said below
Outputs:
- scores: float32 [16384, 128], P('blk', 'expert')
The draws below stay inside these ranges and needn't reach their ends.
Inputs may be any that keep to these rules, and one draw needn't show every extreme that they name: counts of tokens of one example, 0 where the expert gets none of them. Each expert's factor has the largest entry of each row on its diagonal.
All inputs are finite; a program needn't handle non-finite values.
Results may differ from the reference program's by a relative error of at most 0.0038.
Values may be sent and summed in bfloat16 or wider, within the bound.
A program may use at most 64 MiB of HBM per device.

```python
import math
import jax
import jax.numpy as jnp
from jax import lax

K = 2304
TOKS_EX = 64
EXPERTS = 2
Q_ALL = 16384
T_ALL = 128


def draw_factor(key, part):
    base = jax.random.fold_in(key, 7)
    noise_key, scale_key = jax.random.split(base, 2)
    noise = jax.random.normal(noise_key, (EXPERTS, K, K), jnp.float32) * (0.5 / math.sqrt(K))
    row_scales = jnp.exp(jax.random.uniform(scale_key, (EXPERTS, K, 1), jnp.float32, math.log(0.4), math.log(2.5)))
    identity = jnp.eye(K, dtype=jnp.float32)[None, :, :]
    return (row_scales * (identity + noise)).astype(jnp.bfloat16)


def place_ends(array, stream_key, low, high):
    dims = array.shape
    index_at = [jax.random.randint(jax.random.fold_in(stream_key, axis), (), 0, dims[axis]) for axis in range(len(dims))]
    array = array.at[tuple(index_at)].set(low)
    longest = dims.index(max(dims))
    index_at[longest] = (index_at[longest] + 1) % dims[longest]
    return array.at[tuple(index_at)].set(high)


def steps_of(stream_key, extent, cuts, low, largest):
    level, own = 1.0, jax.random.fold_in(stream_key, 6)
    for axis_at, shards_of in cuts:
        heights = jnp.exp(jax.random.uniform(jax.random.fold_in(own, axis_at), (shards_of,), jnp.float32, low / len(cuts), largest / len(cuts)))
        level = level * jnp.repeat(heights, extent[axis_at] // shards_of).reshape([-1 if axis == axis_at else 1 for axis in range(len(extent))])
    return level


def bell_draw(own_key, extent, deviation, most, shards=(), held_as=jnp.bfloat16):
    level = steps_of(own_key, extent, shards, -0.22, 0.18) if shards else 1.0
    array = jax.random.normal(own_key, extent, jnp.float32) * deviation * level
    return jnp.minimum(jnp.maximum(array, -most), most).astype(held_as)


def setup_inputs(seed: int = 0) -> dict:
    arg_keys = jax.random.split(jax.random.key(seed), 5)
    return {
        "query_grads": bell_draw(arg_keys[0], (EXPERTS, Q_ALL, K), K ** -0.5, 0.125, ((0, 2), (1, 16))),
        "train_grads": bell_draw(arg_keys[1], (EXPERTS, T_ALL, K), 1.0, 6.0, ((0, 2), (1, 16))),
        "counts": place_ends(jax.random.randint(arg_keys[2], (EXPERTS, T_ALL), 0, TOKS_EX + 1), jax.random.fold_in(arg_keys[2], 1), 0, TOKS_EX).astype(jnp.int32),
        "factor": draw_factor(jax.random.fold_in(arg_keys[4], 71), 0),
    }


def reference(query_grads, train_grads, counts, factor):
    def add_expert(totals, inputs):
        query_rows, train_rows, count_row, factor_block = inputs
        pre_train = jnp.dot(train_rows, factor_block, preferred_element_type=jnp.float32).astype(jnp.bfloat16)
        kernel = jnp.dot(pre_train, factor_block.T, preferred_element_type=jnp.float32).astype(jnp.bfloat16)
        products = jnp.dot(query_rows, kernel.T, preferred_element_type=jnp.float32)
        weights = count_row.astype(jnp.float32) / TOKS_EX
        return totals + products * weights[None, :], None

    initial = jnp.zeros((Q_ALL, T_ALL), jnp.float32)
    scores, unused = lax.scan(add_expert, initial, (query_grads, train_grads, counts, factor))
    return scores
```

```python
import functools

import jax
import jax.numpy as jnp
from jax import lax
from jax.experimental import pallas as pl
from jax.experimental.pallas import tpu as pltpu
from jax.sharding import PartitionSpec as P

TOKS_EX = 64
MESH = pl.DeviceIdType.MESH
NT = (((1,), (1,)), ((), ()))
PIECES = 3
CHUNKS = 4


def kernel(
    n_exp, n_chip,
    counts_ref, train_ref, query_hbm, factor_hbm, out_ref,
    query, factor, train_out, train_in, part, part_out, part_in, near_in,
    pre_out, pre_in, ker, kmat, early, score, score_out, score_in,
    query_sem, own_sem, pair_send, pair_recv,
    a_send, a_recv, b_send, b_recv, c_send, c_recv, d_send, d_recv,
    f_send, f_recv, e_send, e_recv,
):
    expert, blk = lax.axis_index("expert"), lax.axis_index("blk")
    chip, core = blk // 2, blk % 2
    mate = chip * 2 + (1 - core)
    peers = [lax.rem(chip + k, n_chip) for k in range(1, n_chip)]
    rivals = [lax.rem(expert + k, n_exp) for k in range(1, n_exp)]
    t_loc, depth = train_ref.shape[0], factor_hbm.shape[0]
    width = factor_hbm.shape[1]
    t_plane = t_loc * n_chip
    wide = 2 * depth

    barrier = pltpu.get_barrier_semaphore()
    for peer in peers:
        pl.semaphore_signal(barrier, inc=1, device_id=(expert, peer * 2 + core), device_id_type=MESH)
    pl.semaphore_signal(barrier, inc=1, device_id=(expert, mate), device_id_type=MESH)
    for rival in rivals:
        pl.semaphore_signal(barrier, inc=1, device_id=(rival, blk), device_id_type=MESH)
    own_copy = pltpu.make_async_copy(factor_hbm, factor.at[core], own_sem)
    own_copy.start()
    query_copy = pltpu.make_async_copy(query_hbm, query, query_sem)
    query_copy.start()

    train = train_ref[...].astype(jnp.float32)
    for c in range(n_chip):
        train_out[c] = train[:, c * wide:(c + 1) * wide].astype(jnp.bfloat16)
    pl.semaphore_wait(barrier, n_chip - 1 + 1 + n_exp - 1)

    def to_peers(source, target, send, recv):
        copies = []
        for k, peer in enumerate(peers):
            copy = pltpu.make_async_remote_copy(
                src_ref=source(peer), dst_ref=target(chip), send_sem=send(k),
                recv_sem=recv(chip), device_id=(expert, peer * 2 + core), device_id_type=MESH,
            )
            copy.start()
            copies.append(copy)
        return copies

    def from_peer(source, target, send, recv, k):
        peer = peers[k]
        pltpu.make_async_remote_copy(
            src_ref=source(peer), dst_ref=target(peer), send_sem=send(k),
            recv_sem=recv(peer), device_id=(expert, peer * 2 + core), device_id_type=MESH,
        ).wait_recv()

    a_args = (lambda c: train_out.at[c], lambda c: train_in.at[c], lambda k: a_send.at[k], lambda c: a_recv.at[c])
    a_copies = to_peers(*a_args)
    pair_copy = pltpu.make_async_remote_copy(
        src_ref=factor_hbm, dst_ref=factor.at[core], send_sem=pair_send, recv_sem=pair_recv,
        device_id=(expert, mate), device_id_type=MESH,
    )
    pair_copy.start()
    train_in[chip] = train_out[chip]
    own_copy.wait()
    pair_copy.wait_recv()
    for k in range(n_chip - 1):
        from_peer(*a_args, k)

    rows = train_in[...].astype(jnp.float32).reshape(t_plane, wide)
    first = rows[:, :depth].astype(jnp.bfloat16)
    second = rows[:, depth:].astype(jnp.bfloat16)
    half_chips = n_chip // 2
    base = chip // half_chips * half_chips
    near = [base + lax.rem(chip - base + k, half_chips) for k in range(1, half_chips)]
    far = [n_chip - half_chips - base + lax.rem(chip - base + k, half_chips) for k in range(half_chips)]
    order = [(peer, part_out, part_in) for peer in far] + [(peer, part, near_in) for peer in near]
    span = width // PIECES
    pieces = [slice(s * span, (s + 1) * span) for s in range(PIECES)]

    def share_copy(k, s, slot, peer, source, target):
        return pltpu.make_async_remote_copy(
            src_ref=source.at[peer, :, pieces[s]], dst_ref=target.at[slot, :, pieces[s]], send_sem=b_send.at[k, s],
            recv_sem=b_recv.at[slot, s], device_id=(expert, peer * 2 + core), device_id_type=MESH,
        )

    b_copies = []
    for s, cols in enumerate(pieces):
        share = jnp.dot(first, factor[0, :, cols], preferred_element_type=jnp.float32)
        share = share + jnp.dot(second, factor[1, :, cols], preferred_element_type=jnp.float32)
        share = share.reshape(n_chip, t_loc, span)
        part[:, :, cols] = share
        part_out[:, :, cols] = share.astype(jnp.bfloat16)
        for k, entry in enumerate(order):
            copy = share_copy(k, s, chip, *entry)
            copy.start()
            b_copies.append(copy)

    at_row = lax.broadcasted_iota(jnp.int32, (t_loc, span), 0)
    weight = jnp.zeros((t_loc, span), jnp.float32)
    for i in range(t_loc):
        weight = jnp.where(at_row == i, counts_ref[0, i].astype(jnp.float32) / TOKS_EX, weight)

    def c_args(s):
        return (
            lambda c: pre_out.at[:, pieces[s]], lambda c: pre_in.at[c, :, pieces[s]],
            lambda k: c_send.at[k, s], lambda c: c_recv.at[c, s],
        )

    c_copies = []
    for s, cols in enumerate(pieces):
        total = part[chip, :, cols]
        for k, (peer, source, target) in reversed(list(enumerate(order))):
            share_copy(k, s, peer, peer, source, target).wait_recv()
            total = total + target[peer, :, cols].astype(jnp.float32)
        pre_out[:, cols] = (total * weight).astype(jnp.bfloat16)
        c_copies += to_peers(*c_args(s))
        pre_in[chip, :, cols] = pre_out[:, cols]

    halves = [None, None]
    for s, cols in enumerate(pieces):
        for k in range(n_chip - 1):
            from_peer(*c_args(s), k)
        pre = pre_in[:, :, cols].astype(jnp.float32).reshape(t_plane, span).astype(jnp.bfloat16)
        for c in range(2):
            more = lax.dot_general(factor[c, :, cols], pre, NT, preferred_element_type=jnp.float32)
            halves[c] = more if halves[c] is None else halves[c] + more
    ker[core, chip] = jnp.concatenate(halves, axis=1).astype(jnp.bfloat16)

    def d_copy(k, peer, slot):
        return pltpu.make_async_remote_copy(
            src_ref=ker.at[core, chip], dst_ref=ker.at[core, slot], send_sem=d_send.at[k],
            recv_sem=d_recv.at[slot], device_id=(expert, peer * 2 + core), device_id_type=MESH,
        )

    d_copies = [d_copy(k, peer, chip) for k, peer in enumerate(peers)]
    for copy in d_copies:
        copy.start()

    def pass_copy(c, plane):
        return pltpu.make_async_remote_copy(
            src_ref=ker.at[plane, c], dst_ref=ker.at[plane, c], send_sem=f_send.at[c],
            recv_sem=f_recv.at[c], device_id=(expert, mate), device_id_type=MESH,
        )

    pass_copy(chip, core).start()
    for copy in a_copies + b_copies + [pair_copy]:
        copy.wait_send()
    step = query.shape[0] // CHUNKS
    t_part = t_plane // n_exp
    half_width = width // 2
    e_copies = []

    def arrive(plane, group):
        @pl.when(core == plane)
        def own():
            for c in group:
                if c is not chip:
                    d_copy(0, c, c).wait_recv()
                    pass_copy(c, core).start()

        @pl.when(core != plane)
        def other():
            for c in group:
                pass_copy(c, 1 - core).wait_recv()

    def unpack(plane, j, h, group):
        first_chip = (chip // half_chips + h) % 2 * half_chips
        for k in range(half_chips):
            both = ker[plane, first_chip + k].astype(jnp.float32)
            for half in range(2):
                start = (2 * k + half) * depth
                rows = both[:, half * t_plane:(half + 1) * t_plane]
                kmat[j, h, start:start + depth, :] = rows.astype(kmat.dtype)

    def found(j, h, i):
        side = (chip // half_chips + h) % 2
        at = pl.ds(pl.multiple_of(side * half_width, half_width), half_width)
        return jnp.dot(
            query[i * step:(i + 1) * step, at], kmat[j, h].astype(jnp.bfloat16), preferred_element_type=jnp.float32
        )

    sides = ([chip] + near, far)
    for j, plane in enumerate((1, 0)):
        for h, group in enumerate(sides):
            arrive(plane, group)
            unpack(plane, j, h, group)
            if j == 0 and h == 0:
                query_copy.wait()
            for i in range(CHUNKS):
                if h == 0:
                    early[i] = found(j, h, i)
                    continue
                whole = (early[i] + found(j, h, i)).T
                for g in range(n_exp):
                    block = whole[g * t_part:(g + 1) * t_part, :]
                    score[j, g, i] = block
                    score_out[j, g, i] = block.astype(jnp.bfloat16)
                for k, rival in enumerate(rivals):
                    copy = pltpu.make_async_remote_copy(
                        src_ref=score_out.at[j, rival, i], dst_ref=score_in.at[j, expert, i],
                        send_sem=e_send.at[k, j, i], recv_sem=e_recv.at[expert, j, i],
                        device_id=(rival, blk), device_id_type=MESH,
                    )
                    copy.start()
                    e_copies.append(copy)
    for copy in c_copies + d_copies:
        copy.wait_send()
    for c in range(n_chip):
        pass_copy(c, core).wait_send()

    for j, plane in enumerate((1, 0)):
        for i in range(CHUNKS):
            total = score[j, expert, i]
            for k, rival in enumerate(rivals):
                pltpu.make_async_remote_copy(
                    src_ref=score_out.at[j, rival, i], dst_ref=score_in.at[j, rival, i],
                    send_sem=e_send.at[k, j, i], recv_sem=e_recv.at[rival, j, i],
                    device_id=(rival, blk), device_id_type=MESH,
                ).wait_recv()
                total = total + score_in[j, rival, i].astype(jnp.float32)
            for c in range(t_part // t_loc):
                at = (2 * c + plane) * t_loc
                out_ref[at:at + t_loc, i * step:(i + 1) * step] = total[c * t_loc:(c + 1) * t_loc, :]
    for copy in e_copies:
        copy.wait_send()


def on_device(n_exp, n_blk, query_grads, train_grads, counts, factor):
    n_chip = n_blk // 2
    query_grads, train_grads, factor = query_grads[0], train_grads[0], factor[0]
    q_loc, width = query_grads.shape
    t_loc, depth = train_grads.shape[0], factor.shape[0]
    t_plane = t_loc * n_chip
    t_part = t_plane // n_exp
    bf16, f32 = jnp.bfloat16, jnp.float32
    vmem = pl.BlockSpec(memory_space=pltpu.VMEM)
    hbm = pl.BlockSpec(memory_space=pl.ANY)
    dma = pltpu.SemaphoreType.DMA
    transposed = pl.pallas_call(
        functools.partial(kernel, n_exp, n_chip),
        out_shape=pltpu.VMEM((2 * t_part, q_loc), f32),
        in_specs=[pl.BlockSpec(memory_space=pltpu.SMEM), vmem, hbm, hbm],
        out_specs=vmem,
        scratch_shapes=[
            pltpu.VMEM((q_loc, width), bf16),
            pltpu.VMEM((2, depth, width), bf16),
            pltpu.VMEM((n_chip, t_loc, 2 * depth), bf16),
            pltpu.VMEM((n_chip, t_loc, 2 * depth), bf16),
            pltpu.VMEM((n_chip, t_loc, width), f32),
            pltpu.VMEM((n_chip, t_loc, width), bf16),
            pltpu.VMEM((n_chip, t_loc, width), bf16),
            pltpu.VMEM((n_chip, t_loc, width), f32),
            pltpu.VMEM((t_loc, width), bf16),
            pltpu.VMEM((n_chip, t_loc, width), bf16),
            pltpu.VMEM((2, n_chip, depth, 2 * t_plane), bf16),
            pltpu.VMEM((2, 2, width // 2, t_plane), bf16 if depth % 16 == 0 else f32),
            pltpu.VMEM((CHUNKS, q_loc // CHUNKS, t_plane), f32),
            pltpu.VMEM((2, n_exp, CHUNKS, t_part, q_loc // CHUNKS), f32),
            pltpu.VMEM((2, n_exp, CHUNKS, t_part, q_loc // CHUNKS), bf16),
            pltpu.VMEM((2, n_exp, CHUNKS, t_part, q_loc // CHUNKS), bf16),
            dma, dma, dma, dma,
            dma((n_chip,)), dma((n_chip,)), dma((n_chip, PIECES)), dma((n_chip, PIECES)),
            dma((n_chip, PIECES)), dma((n_chip, PIECES)), dma((n_chip,)), dma((n_chip,)),
            dma((n_chip,)), dma((n_chip,)), dma((n_exp, 2, CHUNKS)), dma((n_exp, 2, CHUNKS)),
        ],
        compiler_params=pltpu.CompilerParams(collective_id=0, has_side_effects=True),
        name="influence",
    )(counts, train_grads, query_grads, factor)
    return transposed.T


def solution(mesh):
    return jax.shard_map(
        functools.partial(on_device, mesh.shape["expert"], mesh.shape["blk"]),
        mesh=mesh,
        in_specs=(
            P("expert", "blk", None),
            P("expert", "blk", None),
            P("expert", "blk"),
            P("expert", "blk", None),
        ),
        out_specs=P("blk", "expert"),
        check_vma=False,
    )
```
